32 devices in a mesh: groups: 2 (over x), blk: 8 (over z, y), head: 2 (over core).
Axes of the slice: x: 2, y: 2, z: 4, core: 2. Of those that a mesh axis runs over, the one named last changes fastest.
Arguments:
- q_latent: float32 [32, 128, 512], P(('groups', 'blk'), 'head'), parts along dimension 0, may hold values from -16 to 16
- q_rope: float32 [32, 128, 64], P(('groups', 'blk'), 'head'), parts along dimension 0, may hold values from -8 to 8
- cache_latent: float32 [32768, 512], P(('groups', 'blk')), parts along dimension 0, may hold values from -8 to 8
- cache_rope: float32 [32768, 64], P(('groups', 'blk')), parts along dimension 0, may hold values from -4 to 4
- home_offset: int32 [32], P(('groups', 'blk')), parts along dimension 0, may hold values from 0 to 14335
- lengths: int32 [32], P(('groups', 'blk')), parts along dimension 0, may hold values from 1 to 14336, as said below
Outputs:
- attended: float32 [32, 128, 512], P(('groups', 'blk'), 'head'), parts along dimension 0
The draws below stay inside these ranges and needn't reach their ends.
There are 2 independent parts, one for each index of `groups`. The reference program is written for one: setup_inputs(seed, part) draws one part's arguments, and reference() takes and returns one part's arrays. A program takes and returns all parts, laid end to end along the dimension named above; each array names one. Nothing has to cross between parts.
Inputs may be any that keep to these rules, and one draw needn't show every extreme that they name: `lengths`: some query has all 14336 cells live.
All inputs are finite; a program needn't handle non-finite values.
Results may differ from the reference program's by a relative error of at most 0.0003.
Values sent between devices are 32-bit elements; how exact they have to be, the bound alone decides.
A program may use at most 64 MiB of HBM per device.

```python
import math
import jax
import jax.numpy as jnp
from jax import lax

LAT = 512
ROPE = 64
NOPE = 128
HEADS = 128
QDEV = 2
CACHE_DEV = 2048
HOPS = 3
BATCH = 16
SEQ = 16384
WINDOW = 14336


def layout(base_key):
    int_key = jax.random.fold_in(base_key, 7)
    beginnings = jax.random.randint(jax.random.fold_in(int_key, 1), (BATCH,), 0, WINDOW)
    extents = jax.random.randint(jax.random.fold_in(int_key, 2), (BATCH,), 1, WINDOW + 1)
    chosen = jax.random.randint(jax.random.fold_in(int_key, 3), (), 0, BATCH)
    query_ids = jnp.arange(BATCH)
    extents = jnp.where(query_ids == chosen, WINDOW, extents)
    return (beginnings.astype(jnp.int32), extents.astype(jnp.int32))


def tables(base_key):
    latent_key = jax.random.fold_in(base_key, 21)
    rotary_key = jax.random.fold_in(base_key, 22)
    latent = jax.random.truncated_normal(latent_key, -4.0, 4.0, (SEQ, LAT), jnp.float32)
    rotary = jax.random.truncated_normal(rotary_key, -4.0, 4.0, (SEQ, ROPE), jnp.float32)
    return (latent, rotary)


def draw_cache_latent(key, part):
    return tables(key)[0]


def draw_cache_rope(key, part):
    return tables(key)[1]


def draw_home_offset(key, part):
    return layout(key)[0]


def draw_lengths(key, part):
    return layout(key)[1]


def draw_q_latent(key, part):
    query_key = jax.random.fold_in(key, 31)
    queries = 2.0 * jax.random.truncated_normal(query_key, -4.0, 4.0, (BATCH, HEADS, LAT), jnp.float32)
    return queries


def draw_q_rope(key, part):
    query_key = jax.random.fold_in(key, 32)
    queries = 2.0 * jax.random.truncated_normal(query_key, -4.0, 4.0, (BATCH, HEADS, ROPE), jnp.float32)
    return queries


def setup_inputs(seed: int = 0, part: int = 0) -> dict:
    streams_of = jax.random.split(jax.random.key(seed), 7)
    part_keys = jax.random.split(jax.random.fold_in(streams_of[6], part), 7)
    q_latent = draw_q_latent(jax.random.fold_in(jax.random.fold_in(streams_of[6], part), 71), part)
    q_rope = draw_q_rope(jax.random.fold_in(jax.random.fold_in(streams_of[6], part), 71), part)
    cache_latent = draw_cache_latent(jax.random.fold_in(jax.random.fold_in(streams_of[6], part), 71), part)
    cache_rope = draw_cache_rope(jax.random.fold_in(jax.random.fold_in(streams_of[6], part), 71), part)
    home_offset = draw_home_offset(jax.random.fold_in(jax.random.fold_in(streams_of[6], part), 71), part)
    lengths = draw_lengths(jax.random.fold_in(jax.random.fold_in(streams_of[6], part), 71), part)
    return {"q_latent": q_latent, "q_rope": q_rope, "cache_latent": cache_latent, "cache_rope": cache_rope, "home_offset": home_offset, "lengths": lengths}


def reference(q_latent, q_rope, cache_latent, cache_rope, home_offset, lengths):
    scale = 1.0 / math.sqrt(NOPE + ROPE)
    offsets = jnp.arange(WINDOW, dtype=jnp.int32)

    def attend_one(packed):
        query, query_rope, index, beginning, extent = packed
        first_block = index // QDEV - HOPS
        positions = jnp.mod(first_block * CACHE_DEV + offsets, SEQ).astype(jnp.int32)
        keys = jnp.take(cache_latent, positions, axis=0)
        rope_keys = jnp.take(cache_rope, positions, axis=0)
        scores = (jnp.dot(query, keys.T, precision=lax.Precision.HIGHEST) + jnp.dot(query_rope, rope_keys.T, precision=lax.Precision.HIGHEST)) * scale
        validity = jnp.mod(offsets - beginning, WINDOW) < extent
        peak = lax.optimization_barrier(jnp.max(jnp.where(validity[None, :], scores, -jnp.inf), axis=1, keepdims=True))
        weights = jnp.where(validity[None, :], jnp.exp(scores - peak), 0.0)
        totals = lax.optimization_barrier(jnp.sum(weights, axis=1, keepdims=True))
        return jnp.dot(weights, keys, precision=lax.Precision.HIGHEST) / totals
    indices = jnp.arange(BATCH, dtype=jnp.int32)
    return lax.map(attend_one, (q_latent, q_rope, indices, home_offset, lengths))
```

```python
import functools
import math

import jax
import jax.numpy as jnp
from jax import lax
from jax.experimental import pallas as pl
from jax.experimental.pallas import tpu as pltpu
from jax.sharding import PartitionSpec as P

ROPE = 64
NOPE = 128
HOPS = 3

MESH = pl.DeviceIdType.MESH
FLOOR = -1e30
DEAD = -2e30
FACTOR = math.log2(math.e) / math.sqrt(NOPE + ROPE)
CHUNK = 512

NT = (((1,), (1,)), ((), ()))


def split(x):
    high = x.astype(jnp.bfloat16)
    low = (x - high.astype(jnp.float32)).astype(jnp.bfloat16)
    return high, low


def prepare_cache(cache_ref, rope_ref, kcat, vt_hi, vt_lo):
    cells, width = cache_ref.shape
    step = 256

    def body(i, _):
        rows = pl.ds(pl.multiple_of(i * step, step), step)
        block = cache_ref[rows, :]
        high, low = split(block)
        kcat[rows, 0:width] = high
        kcat[rows, width : 2 * width] = low
        turned = block.T
        t_high, t_low = split(turned)
        vt_hi[:, rows] = t_high
        vt_lo[:, rows] = t_low
        rope = rope_ref[rows, :]
        r_high = rope.astype(jnp.bfloat16).astype(jnp.float32)
        r_low = rope - r_high
        wide = jnp.concatenate([r_high, r_high, r_low, jnp.zeros_like(rope)], axis=1)
        kcat[rows, 2 * width : 2 * width + 4 * rope.shape[1]] = wide.astype(jnp.bfloat16)
        return 0

    lax.fori_loop(0, cells // step, body, 0)


def rope_rows(aux, heads):
    packed = aux[0:heads, :] * FACTOR
    high = packed.astype(jnp.bfloat16).astype(jnp.float32)
    low = packed - high
    half = packed.shape[1] // 2
    blank = jnp.zeros((heads, half), jnp.float32)
    rows = []
    for part in (slice(0, half), slice(half, 2 * half)):
        rows.append(jnp.concatenate([high[:, part], low[:, part], high[:, part], blank], axis=1))
    return jnp.concatenate(rows, axis=0).astype(jnp.bfloat16)


def visit(parts, kcat, vt_hi, vt_lo, s_ref, ph_ref, pl_ref, window):
    cells = kcat.shape[0]
    width = vt_hi.shape[0]
    heads = parts[0][1].shape[0] - 8
    query = jnp.concatenate([p[0] for p in parts], axis=0) * FACTOR
    q_hi, q_lo = split(query)
    rope = jnp.concatenate([rope_rows(p[1], heads) for p in parts], axis=0)
    q_cat = jnp.concatenate([q_hi, q_hi, rope], axis=1)
    starts = jnp.concatenate([p[1][heads : heads + 1, :] - p[2] for p in parts], axis=1)
    extents = jnp.concatenate([p[1][heads + 1 : heads + 2, :] for p in parts], axis=1)
    ends = starts + extents
    wrapped = ends - window
    count = query.shape[0]
    peak = jnp.full((1, count), FLOOR, jnp.float32)
    for c in range(cells // CHUNK):
        rows = slice(c * CHUNK, (c + 1) * CHUNK)
        scores = lax.dot_general(kcat[rows, :], q_cat, NT, preferred_element_type=jnp.float32)
        scores += lax.dot_general(
            kcat[rows, 0:width], q_lo, NT, preferred_element_type=jnp.float32
        )
        cell = lax.broadcasted_iota(jnp.int32, (CHUNK, count), 0).astype(jnp.float32) + c * CHUNK
        live = ((cell >= starts) & (cell < ends)) | (cell < wrapped)
        scores = jnp.where(live, scores, DEAD)
        s_ref[rows, 0:count] = scores
        peak = jnp.maximum(peak, jnp.max(scores, axis=0, keepdims=True))
    total = jnp.zeros((1, count), jnp.float32)
    summed = None
    for c in range(cells // CHUNK):
        rows = slice(c * CHUNK, (c + 1) * CHUNK)
        weights = jnp.exp2(s_ref[rows, 0:count] - peak)
        total += jnp.sum(weights, axis=0, keepdims=True)
        high, low = split(weights)
        ph_ref[rows, 0:count] = high
        pl_ref[rows, 0:count] = low
    high = ph_ref[:, 0:count]
    summed = jnp.dot(vt_hi[...], high, preferred_element_type=jnp.float32)
    summed += jnp.dot(vt_hi[...], pl_ref[:, 0:count], preferred_element_type=jnp.float32)
    summed += jnp.dot(vt_lo[...], high, preferred_element_type=jnp.float32)
    return summed, peak, total


def window_kernel(
    size,
    q_ref, aux_ref, cache_ref, rope_ref, out_ref,
    kcat, vt_hi, vt_lo, s_ref, ph_ref, pl_ref,
    q_got, aux_got, sums, stats, sums_got, stats_got,
    q_send, q_recv, a_send, a_recv, o_send, o_recv, t_send, t_recv,
):
    me = lax.axis_index("blk")
    cells = cache_ref.shape[0]
    window = (2 * HOPS + 1) * cells
    distances = [sign * k for k in range(1, HOPS + 1) for sign in (1, -1)]

    def device(distance):
        return {"blk": lax.rem(me + distance + size, size)}

    barrier = pltpu.get_barrier_semaphore()
    for d in distances:
        pl.semaphore_signal(barrier, inc=1, device_id=device(d), device_id_type=MESH)
    pl.semaphore_wait(barrier, 2 * HOPS)

    sent = []
    for i, d in enumerate(distances):
        for source, target, send, recv in (
            (q_ref, q_got, q_send, q_recv),
            (aux_ref, aux_got, a_send, a_recv),
        ):
            copy = pltpu.make_async_remote_copy(
                src_ref=source, dst_ref=target.at[i], send_sem=send.at[i], recv_sem=recv.at[i],
                device_id=device(d), device_id_type=MESH,
            )
            copy.start()
            sent.append(copy)

    prepare_cache(cache_ref, rope_ref, kcat, vt_hi, vt_lo)
    run = functools.partial(
        visit, kcat=kcat, vt_hi=vt_hi, vt_lo=vt_lo, s_ref=s_ref, ph_ref=ph_ref, pl_ref=pl_ref,
        window=window,
    )
    rows = q_ref.shape[0]
    own = run([(q_ref[...], aux_ref[...], float(HOPS * cells))])
    sums[2 * HOPS, :, :] = own[0]
    stats[2 * HOPS, 0:1, :] = own[1]
    stats[2 * HOPS, 1:2, :] = own[2]

    def pair(k, _):
        parts = []
        for j, sign in ((0, 1), (1, -1)):
            i = 2 * k + j
            for source, target, send, recv in (
                (q_ref, q_got, q_send, q_recv),
                (aux_ref, aux_got, a_send, a_recv),
            ):
                pltpu.make_async_remote_copy(
                    src_ref=source, dst_ref=target.at[i], send_sem=send.at[i], recv_sem=recv.at[i],
                    device_id=device(1), device_id_type=MESH,
                ).wait_recv()
            slot = HOPS + sign * (k + 1)
            parts.append((q_got[i], aux_got[i], (slot * cells).astype(jnp.float32)))
        summed, peak, total = run(parts)
        for j, sign in ((0, 1), (1, -1)):
            i = 2 * k + j
            lanes = slice(j * rows, (j + 1) * rows)
            sums[i, :, :] = summed[:, lanes]
            stats[i, 0:1, :] = peak[:, lanes]
            stats[i, 1:2, :] = total[:, lanes]
            for source, target, send, recv in (
                (sums, sums_got, o_send, o_recv),
                (stats, stats_got, t_send, t_recv),
            ):
                pltpu.make_async_remote_copy(
                    src_ref=source.at[i], dst_ref=target.at[i],
                    send_sem=send.at[i], recv_sem=recv.at[i],
                    device_id=device(-sign * (k + 1)), device_id_type=MESH,
                ).start()
        return 0

    lax.fori_loop(0, HOPS, pair, 0)

    for i in range(2 * HOPS):
        for source, target, send, recv in (
            (sums, sums_got, o_send, o_recv),
            (stats, stats_got, t_send, t_recv),
        ):
            copy = pltpu.make_async_remote_copy(
                src_ref=source.at[i], dst_ref=target.at[i],
                send_sem=send.at[i], recv_sem=recv.at[i],
                device_id=device(1), device_id_type=MESH,
            )
            copy.wait_recv()
            copy.wait_send()

    for copy in sent:
        copy.wait_send()

    peak = stats[2 * HOPS, 0:1, :]
    for i in range(2 * HOPS):
        peak = jnp.maximum(peak, stats_got[i, 0:1, :])
    factors = [jnp.exp2(stats[2 * HOPS, 0:1, :] - peak)]
    total = stats[2 * HOPS, 1:2, :] * factors[0]
    for i in range(2 * HOPS):
        factors.append(jnp.exp2(stats_got[i, 0:1, :] - peak))
        total += stats_got[i, 1:2, :] * factors[i + 1]
    width = sums.shape[1]
    for c in range(0, width, 128):
        piece = sums[2 * HOPS, c : c + 128, :] * factors[0]
        for i in range(2 * HOPS):
            piece += sums_got[i, c : c + 128, :] * factors[i + 1]
        out_ref[:, c : c + 128] = (piece / total).T


def pack_aux(q_rope, home_offset, lengths):
    height, heads, rope = q_rope.shape
    packed = jnp.concatenate([q_rope[i] for i in range(height)], axis=1)
    meta = jnp.stack([home_offset, lengths]).astype(jnp.float32)
    meta = jnp.repeat(meta, heads, axis=1)
    return jnp.concatenate([packed, meta, jnp.zeros((6, height * heads), jnp.float32)], axis=0)


def shards(size, q_latent, q_rope, cache_latent, cache_rope, home_offset, lengths):
    height, heads, width = q_latent.shape
    cells, rope = cache_rope.shape
    rows = height * heads
    aux = pack_aux(q_rope, home_offset, lengths)
    flat = q_latent.reshape(rows, width)
    n = 2 * HOPS
    dma = pltpu.SemaphoreType.DMA
    out = pl.pallas_call(
        functools.partial(window_kernel, size),
        out_shape=jax.ShapeDtypeStruct((rows, width), jnp.float32),
        in_specs=[pl.BlockSpec(memory_space=pltpu.VMEM)] * 4,
        out_specs=pl.BlockSpec(memory_space=pltpu.VMEM),
        scratch_shapes=[
            pltpu.VMEM((cells, 2 * width + 4 * rope), jnp.bfloat16),
            pltpu.VMEM((width, cells), jnp.bfloat16),
            pltpu.VMEM((width, cells), jnp.bfloat16),
            pltpu.VMEM((cells, 2 * rows), jnp.float32),
            pltpu.VMEM((cells, 2 * rows), jnp.bfloat16),
            pltpu.VMEM((cells, 2 * rows), jnp.bfloat16),
            pltpu.VMEM((n, rows, width), jnp.float32),
            pltpu.VMEM((n, heads + 8, rows), jnp.float32),
            pltpu.VMEM((n + 1, width, rows), jnp.float32),
            pltpu.VMEM((n + 1, 8, rows), jnp.float32),
            pltpu.VMEM((n, width, rows), jnp.float32),
            pltpu.VMEM((n, 8, rows), jnp.float32),
        ]
        + [dma((n,))] * 8,
        compiler_params=pltpu.CompilerParams(
            collective_id=0, has_side_effects=True, vmem_limit_bytes=60 * 1024 * 1024
        ),
    )(flat, aux, cache_latent, cache_rope)
    return out.reshape(height, heads, width)


def solution(mesh):
    return jax.shard_map(
        functools.partial(shards, mesh.shape["blk"]),
        mesh=mesh,
        in_specs=(
            P(("groups", "blk"), "head", None),
            P(("groups", "blk"), "head", None),
            P(("groups", "blk"), None),
            P(("groups", "blk"), None),
            P(("groups", "blk")),
            P(("groups", "blk")),
        ),
        out_specs=P(("groups", "blk"), "head", None),
        check_vma=False,
    )
```

```python
import functools
import math

import jax
import jax.numpy as jnp
from jax import lax
from jax.experimental import pallas as pl
from jax.experimental.pallas import tpu as pltpu
from jax.sharding import PartitionSpec as P

ROPE = 64
NOPE = 128
HOPS = 3

MESH = pl.DeviceIdType.MESH
FLOOR = -1e30
DEAD = -2e30
FACTOR = math.log2(math.e) / math.sqrt(NOPE + ROPE)
CHUNK = 512
STEP = 256
EARLY = 32

NT = (((1,), (1,)), ((), ()))


def split(x):
    high = x.astype(jnp.bfloat16)
    low = (x - high.astype(jnp.float32)).astype(jnp.bfloat16)
    return high, low


def prepare_cache(cache_ref, rope_ref, kcat, vt_hi, vt_lo, fetch=None):
    cells, width = cache_ref.shape
    step = STEP

    def body(i, _):
        if fetch is not None:
            fetch(i).wait()
        rows = pl.ds(pl.multiple_of(i * step, step), step)
        block = cache_ref[rows, :]
        high, low = split(block)
        kcat[rows, 0:width] = high
        kcat[rows, width : 2 * width] = low
        turned = block.T
        t_high, t_low = split(turned)
        vt_hi[:, rows] = t_high
        vt_lo[:, rows] = t_low
        rope = rope_ref[:, rows].T
        r_high = rope.astype(jnp.bfloat16).astype(jnp.float32)
        r_low = rope - r_high
        wide = jnp.concatenate([r_high, r_high, r_low, jnp.zeros_like(rope)], axis=1)
        kcat[rows, 2 * width : 2 * width + 4 * rope.shape[1]] = wide.astype(jnp.bfloat16)
        return 0

    lax.fori_loop(0, cells // step, body, 0)


def rope_rows(aux, heads):
    packed = aux[0:heads, :] * FACTOR
    high = packed.astype(jnp.bfloat16).astype(jnp.float32)
    low = packed - high
    half = packed.shape[1] // 2
    blank = jnp.zeros((heads, half), jnp.float32)
    rows = []
    for part in (slice(0, half), slice(half, 2 * half)):
        rows.append(jnp.concatenate([high[:, part], low[:, part], high[:, part], blank], axis=1))
    return jnp.concatenate(rows, axis=0).astype(jnp.bfloat16)


def visit(parts, kcat, vt_hi, vt_lo, s_ref, ph_ref, pl_ref, window):
    cells = kcat.shape[0]
    width = vt_hi.shape[0]
    heads = parts[0][1].shape[0] - 8
    query = jnp.concatenate([p[0] for p in parts], axis=0) * FACTOR
    q_hi, q_lo = split(query)
    rope = jnp.concatenate([rope_rows(p[1], heads) for p in parts], axis=0)
    q_cat = jnp.concatenate([q_hi, q_hi, rope], axis=1)
    starts = jnp.concatenate([p[1][heads : heads + 1, :] - p[2] for p in parts], axis=1)
    extents = jnp.concatenate([p[1][heads + 1 : heads + 2, :] * p[3] for p in parts], axis=1)
    ends = starts + extents
    wrapped = ends - window
    count = query.shape[0]
    peak = jnp.full((1, count), FLOOR, jnp.float32)
    for c in range(cells // CHUNK):
        rows = slice(c * CHUNK, (c + 1) * CHUNK)
        scores = lax.dot_general(kcat[rows, :], q_cat, NT, preferred_element_type=jnp.float32)
        scores += lax.dot_general(
            kcat[rows, 0:width], q_lo, NT, preferred_element_type=jnp.float32
        )
        cell = lax.broadcasted_iota(jnp.int32, (CHUNK, count), 0).astype(jnp.float32) + c * CHUNK
        live = ((cell >= starts) & (cell < ends)) | (cell < wrapped)
        scores = jnp.where(live, scores, DEAD)
        s_ref[rows, 0:count] = scores
        peak = jnp.maximum(peak, jnp.max(scores, axis=0, keepdims=True))
    total = jnp.zeros((1, count), jnp.float32)
    summed = None
    for c in range(cells // CHUNK):
        rows = slice(c * CHUNK, (c + 1) * CHUNK)
        weights = jnp.exp2(s_ref[rows, 0:count] - peak)
        total += jnp.sum(weights, axis=0, keepdims=True)
        high, low = split(weights)
        ph_ref[rows, 0:count] = high
        pl_ref[rows, 0:count] = low
    high = ph_ref[:, 0:count]
    summed = jnp.dot(vt_hi[...], high, preferred_element_type=jnp.float32)
    summed += jnp.dot(vt_hi[...], pl_ref[:, 0:count], preferred_element_type=jnp.float32)
    summed += jnp.dot(vt_lo[...], high, preferred_element_type=jnp.float32)
    return summed, peak, total


def window_kernel(
    size,
    q_ref, aux_ref, cache_ref, rope_ref, out_ref,
    kcat, vt_hi, vt_lo, s_ref, ph_ref, pl_ref,
    q_got, aux_got, sums, stats, sums_got, stats_got,
    q_send, q_recv, a_send, a_recv, o_send, o_recv, t_send, t_recv,
):
    me = lax.axis_index("blk")
    cells = cache_ref.shape[0]
    window = (2 * HOPS + 1) * cells
    distances = [sign * k for k in range(1, HOPS + 1) for sign in (1, -1)]

    def device(distance):
        return {"blk": lax.rem(me + distance + size, size)}

    barrier = pltpu.get_barrier_semaphore()
    for d in distances:
        pl.semaphore_signal(barrier, inc=1, device_id=device(d), device_id_type=MESH)
    pl.semaphore_wait(barrier, 2 * HOPS)

    sent = []
    for i, d in enumerate(distances):
        for source, target, send, recv in (
            (q_ref, q_got, q_send, q_recv),
            (aux_ref, aux_got, a_send, a_recv),
        ):
            copy = pltpu.make_async_remote_copy(
                src_ref=source, dst_ref=target.at[i], send_sem=send.at[i], recv_sem=recv.at[i],
                device_id=device(d), device_id_type=MESH,
            )
            copy.start()
            sent.append(copy)

    prepare_cache(cache_ref, rope_ref, kcat, vt_hi, vt_lo)
    run = functools.partial(
        visit, kcat=kcat, vt_hi=vt_hi, vt_lo=vt_lo, s_ref=s_ref, ph_ref=ph_ref, pl_ref=pl_ref,
        window=window,
    )
    rows = q_ref.shape[0]
    own = run([(q_ref[...], aux_ref[...], float(HOPS * cells), 1.0)])
    sums[2 * HOPS, :, :] = own[0]
    stats[2 * HOPS, 0:1, :] = own[1]
    stats[2 * HOPS, 1:2, :] = own[2]

    def pair(k, _):
        parts = []
        for j, sign in ((0, 1), (1, -1)):
            i = 2 * k + j
            for source, target, send, recv in (
                (q_ref, q_got, q_send, q_recv),
                (aux_ref, aux_got, a_send, a_recv),
            ):
                pltpu.make_async_remote_copy(
                    src_ref=source, dst_ref=target.at[i], send_sem=send.at[i], recv_sem=recv.at[i],
                    device_id=device(1), device_id_type=MESH,
                ).wait_recv()
            slot = HOPS + sign * (k + 1)
            parts.append((q_got[i], aux_got[i], (slot * cells).astype(jnp.float32), 1.0))
        summed, peak, total = run(parts)
        for j, sign in ((0, 1), (1, -1)):
            i = 2 * k + j
            lanes = slice(j * rows, (j + 1) * rows)
            sums[i, :, :] = summed[:, lanes]
            stats[i, 0:1, :] = peak[:, lanes]
            stats[i, 1:2, :] = total[:, lanes]
            for source, target, send, recv in (
                (sums, sums_got, o_send, o_recv),
                (stats, stats_got, t_send, t_recv),
            ):
                pltpu.make_async_remote_copy(
                    src_ref=source.at[i], dst_ref=target.at[i],
                    send_sem=send.at[i], recv_sem=recv.at[i],
                    device_id=device(-sign * (k + 1)), device_id_type=MESH,
                ).start()
        return 0

    lax.fori_loop(0, HOPS, pair, 0)

    for i in range(2 * HOPS):
        for source, target, send, recv in (
            (sums, sums_got, o_send, o_recv),
            (stats, stats_got, t_send, t_recv),
        ):
            copy = pltpu.make_async_remote_copy(
                src_ref=source.at[i], dst_ref=target.at[i],
                send_sem=send.at[i], recv_sem=recv.at[i],
                device_id=device(1), device_id_type=MESH,
            )
            copy.wait_recv()
            copy.wait_send()

    for copy in sent:
        copy.wait_send()

    peak = stats[2 * HOPS, 0:1, :]
    for i in range(2 * HOPS):
        peak = jnp.maximum(peak, stats_got[i, 0:1, :])
    factors = [jnp.exp2(stats[2 * HOPS, 0:1, :] - peak)]
    total = stats[2 * HOPS, 1:2, :] * factors[0]
    for i in range(2 * HOPS):
        factors.append(jnp.exp2(stats_got[i, 0:1, :] - peak))
        total += stats_got[i, 1:2, :] * factors[i + 1]
    width = sums.shape[1]
    for c in range(0, width, 128):
        piece = sums[2 * HOPS, c : c + 128, :] * factors[0]
        for i in range(2 * HOPS):
            piece += sums_got[i, c : c + 128, :] * factors[i + 1]
        out_ref[:, c : c + 128] = (piece / total).T


def line_kernel(
    size,
    q_ref, aux_ref, cache_hbm, rope_ref, out_ref,
    kcat, vt_hi, vt_lo, s_ref, ph_ref, pl_ref,
    cache, q_all, aux_all, acc, across, across_got, along_got,
    fetch_sem, own_sem,
    qz_s, qz_r, az_s, az_r, qa_s, qa_r, qy_s, qy_r, ay_s, ay_r, early_s,
    oy_s, oy_r, oz_s, oz_r,
):
    me = lax.axis_index("blk")
    count = size // 2
    z, y = me // 2, lax.rem(me, 2)
    cells, width = cache.shape
    rows = q_ref.shape[0]
    window = (2 * HOPS + 1) * cells
    partner = {"blk": me + 1 - 2 * y}

    def at(zz):
        return {"blk": 2 * zz + y}

    def remote(source, target, send, recv, device):
        return pltpu.make_async_remote_copy(
            src_ref=source, dst_ref=target, send_sem=send, recv_sem=recv,
            device_id=device, device_id_type=MESH,
        )

    def source_row(j):
        near = jnp.minimum(z, count - 1 - z)
        both = j < 2 * near
        distance = jnp.where(both, j // 2 + 1, j - near + 1)
        upward = jnp.where(both, lax.rem(j, 2) == 0, z < count - 1 - z)
        return jnp.where(upward, z + distance, z - distance)

    def q_along(zz, side):
        target = at(lax.rem(z + 1 - 2 * side + count, count))
        return (
            remote(q_all.at[zz, 0], q_all.at[zz, 0], qz_s.at[side, zz], qz_r.at[zz], target),
            remote(aux_all.at[zz, 0], aux_all.at[zz, 0], az_s.at[side, zz], az_r.at[zz], target),
        )

    early_rows, late_rows = pl.ds(0, EARLY), pl.ds(EARLY, rows - EARLY)

    def early_along(zz, side):
        piece = q_all.at[zz, 1, early_rows]
        return remote(piece, piece, qa_s.at[side, zz], qa_r.at[zz], at(lax.rem(z + 1 - 2 * side + count, count)))

    def q_across(zz):
        return (
            remote(
                q_all.at[zz, 0, late_rows], q_all.at[zz, 1, late_rows],
                qy_s.at[zz], qy_r.at[zz], partner,
            ),
            remote(aux_all.at[zz, 0], aux_all.at[zz, 1], ay_s.at[zz], ay_r.at[zz], partner),
        )

    def early_across():
        return remote(
            q_all.at[z, 0, early_rows], q_all.at[z, 1, early_rows], early_s.at[0], qa_r.at[z],
            partner,
        )

    def sum_across(zz):
        return remote(across.at[zz], across_got.at[zz], oy_s.at[zz], oy_r.at[zz], partner)

    def sum_along(zz):
        return remote(acc.at[zz], along_got.at[z], oz_s.at[zz], oz_r.at[z], at(zz))

    def sum_from(zz):
        return remote(acc.at[zz], along_got.at[zz], oz_s.at[zz], oz_r.at[zz], at(zz))

    def fetch(i):
        part = pl.ds(pl.multiple_of(i * STEP, STEP), STEP)
        return pltpu.make_async_copy(cache_hbm.at[part], cache.at[part], fetch_sem.at[i])

    own_copies = (
        pltpu.make_async_copy(q_ref, q_all.at[z, 0], own_sem.at[0]),
        pltpu.make_async_copy(aux_ref, aux_all.at[z, 0], own_sem.at[1]),
    )
    for copy in own_copies:
        copy.start()
    for i in range(cells // STEP):
        fetch(i).start()

    barrier = pltpu.get_barrier_semaphore()
    pl.semaphore_signal(barrier, inc=1, device_id=partner, device_id_type=MESH)
    for k in range(1, count):
        other = at(lax.rem(z + k, count))
        pl.semaphore_signal(barrier, inc=1, device_id=other, device_id_type=MESH)
    for copy in own_copies:
        copy.wait()
    pl.semaphore_wait(barrier, count)

    def sides(zz, action):
        @pl.when((z < count - 1) & (zz <= z))
        def _():
            action(0)

        @pl.when((z > 0) & (zz >= z))
        def _():
            action(1)

    def start_along(side, zz):
        for copy in q_along(zz, side):
            copy.start()

    early_across().start()
    sides(z, functools.partial(start_along, zz=z))
    for copy in q_across(z):
        copy.start()

    prepare_cache(cache, rope_ref, kcat, vt_hi, vt_lo, fetch)
    early_across().wait_recv()
    sides(z, lambda side: early_along(z, side).start())

    def pass_on(zz):
        for copy in q_along(zz, 0):
            copy.wait_recv()
        sides(zz, functools.partial(start_along, zz=zz))
        for copy in q_across(zz):
            copy.start()
        early_along(zz, 0).wait_recv()
        sides(zz, lambda side: early_along(zz, side).start())

    def compute(zz):
        for copy in q_across(zz):
            copy.wait_recv()
        parts = []
        for c in range(2):
            block = 2 * zz + (y if c == 0 else 1 - y)
            slot = lax.rem(me - block + HOPS + size, size)
            alive = jnp.where(slot <= 2 * HOPS, 1.0, 0.0).astype(jnp.float32)
            parts.append((q_all[zz, c], aux_all[zz, c], (slot * cells).astype(jnp.float32), alive))
        summed, peak, total = visit(
            parts, kcat, vt_hi, vt_lo, s_ref, ph_ref, pl_ref, window
        )
        for ref, lanes in ((across, slice(rows, 2 * rows)), (acc, slice(0, rows))):
            ref[zz, 0:width, :] = summed[:, lanes]
            ref[zz, width : width + 8, :] = jnp.concatenate(
                [peak[:, lanes], total[:, lanes], jnp.zeros((6, rows), jnp.float32)], axis=0
            )
        sum_across(zz).start()

    def merge(zz, got, k):
        first, second = acc[zz, width : width + 1, :], got[k, width : width + 1, :]
        peak = jnp.maximum(first, second)
        first, second = jnp.exp2(first - peak), jnp.exp2(second - peak)
        total = acc[zz, width + 1 : width + 2, :] * first
        total += got[k, width + 1 : width + 2, :] * second
        acc[zz, 0:width, :] = acc[zz, 0:width, :] * first + got[k, 0:width, :] * second
        acc[zz, width : width + 1, :] = peak
        acc[zz, width + 1 : width + 2, :] = total

    def step(i, _):
        @pl.when(i < count - 1)
        def _():
            pass_on(source_row(i))

        @pl.when(i < count)
        def _():
            compute(jnp.where(i == 0, z, source_row(i - 1)))

        @pl.when(i >= 1)
        def _():
            zz = jnp.where(i == 1, z, source_row(i - 2))
            sum_across(zz).wait_recv()
            merge(zz, across_got, zz)

            @pl.when(i >= 2)
            def _():
                sum_along(zz).start()

        return 0

    lax.fori_loop(0, count + 1, step, 0)

    def gather(j, _):
        zz = source_row(j)
        sum_from(zz).wait_recv()
        merge(z, along_got, zz)
        return 0

    lax.fori_loop(0, count - 1, gather, 0)
    total = acc[z, width + 1 : width + 2, :]
    for c in range(0, width, 128):
        out_ref[:, c : c + 128] = (acc[z, c : c + 128, :] / total).T

    def finish(side, zz):
        for copy in q_along(zz, side):
            copy.wait_send()
        early_along(zz, side).wait_send()

    early_across().wait_send()
    for k in range(count):
        zz = lax.rem(z + k, count)
        sides(zz, functools.partial(finish, zz=zz))
        for copy in q_across(zz):
            copy.wait_send()
        sum_across(zz).wait_send()
        if k > 0:
            sum_along(zz).wait_send()


def pack_aux(q_rope, home_offset, lengths):
    height, heads, rope = q_rope.shape
    packed = jnp.concatenate([q_rope[i] for i in range(height)], axis=1)
    meta = jnp.stack([home_offset, lengths]).astype(jnp.float32)
    meta = jnp.repeat(meta, heads, axis=1)
    return jnp.concatenate([packed, meta, jnp.zeros((6, height * heads), jnp.float32)], axis=0)


def shards(size, q_latent, q_rope, cache_latent, cache_rope, home_offset, lengths):
    height, heads, width = q_latent.shape
    cells, rope = cache_rope.shape
    rows = height * heads
    aux = pack_aux(q_rope, home_offset, lengths)
    flat = q_latent.reshape(rows, width)
    rope_turned = cache_rope.T
    dma = pltpu.SemaphoreType.DMA
    vmem, anywhere = (pl.BlockSpec(memory_space=m) for m in (pltpu.VMEM, pl.ANY))
    working = [
        pltpu.VMEM((cells, 2 * width + 4 * rope), jnp.bfloat16),
        pltpu.VMEM((width, cells), jnp.bfloat16),
        pltpu.VMEM((width, cells), jnp.bfloat16),
        pltpu.VMEM((cells, 2 * rows), jnp.float32),
        pltpu.VMEM((cells, 2 * rows), jnp.bfloat16),
        pltpu.VMEM((cells, 2 * rows), jnp.bfloat16),
    ]
    if size == 2 * HOPS + 2:
        kernel = line_kernel
        n = size // 2
        in_specs = [anywhere, anywhere, anywhere, vmem]
        scratch = [
            pltpu.VMEM((cells, width), jnp.float32),
            pltpu.VMEM((n, 2, rows, width), jnp.float32),
            pltpu.VMEM((n, 2, heads + 8, rows), jnp.float32),
        ]
        scratch += [pltpu.VMEM((n, width + 8, rows), jnp.float32)] * 4
        scratch += [dma((cells // STEP,)), dma((2,))]
        scratch += [dma((2, n)), dma((n,))] * 3 + [dma((n,))] * 4 + [dma((1,))] + [dma((n,))] * 4
    else:
        kernel = window_kernel
        n = 2 * HOPS
        in_specs = [vmem] * 4
        scratch = [
            pltpu.VMEM((n, rows, width), jnp.float32),
            pltpu.VMEM((n, heads + 8, rows), jnp.float32),
            pltpu.VMEM((n + 1, width, rows), jnp.float32),
            pltpu.VMEM((n + 1, 8, rows), jnp.float32),
            pltpu.VMEM((n, width, rows), jnp.float32),
            pltpu.VMEM((n, 8, rows), jnp.float32),
        ] + [dma((n,))] * 8
    out = pl.pallas_call(
        functools.partial(kernel, size),
        out_shape=jax.ShapeDtypeStruct((rows, width), jnp.float32),
        in_specs=in_specs,
        out_specs=vmem,
        scratch_shapes=working + scratch,
        compiler_params=pltpu.CompilerParams(
            collective_id=0, has_side_effects=True, vmem_limit_bytes=60 * 1024 * 1024
        ),
    )(flat, aux, cache_latent, rope_turned)
    return out.reshape(height, heads, width)


def solution(mesh):
    return jax.shard_map(
        functools.partial(shards, mesh.shape["blk"]),
        mesh=mesh,
        in_specs=(
            P(("groups", "blk"), "head", None),
            P(("groups", "blk"), "head", None),
            P(("groups", "blk"), None),
            P(("groups", "blk"), None),
            P(("groups", "blk")),
            P(("groups", "blk")),
        ),
        out_specs=P(("groups", "blk"), "head", None),
        check_vma=False,
    )
```

```python
import functools
import math

import jax
import jax.numpy as jnp
from jax import lax
from jax.experimental import pallas as pl
from jax.experimental.pallas import tpu as pltpu
from jax.sharding import PartitionSpec as P

ROPE = 64
NOPE = 128
HOPS = 3

MESH = pl.DeviceIdType.MESH
FLOOR = -1e30
DEAD = -2e30
FACTOR = math.log2(math.e) / math.sqrt(NOPE + ROPE)
CHUNK = 256
STEP = 256
EARLY = 64

NT = (((1,), (1,)), ((), ()))


def split(x):
    high = x.astype(jnp.bfloat16)
    low = (x - high.astype(jnp.float32)).astype(jnp.bfloat16)
    return high, low


def prepare_cache(cache_ref, rope_ref, kcat, vt_hi, vt_lo, fetch=None):
    cells, width = cache_ref.shape
    step = STEP

    def body(i, _):
        if fetch is not None:
            fetch(i).wait()
        rows = pl.ds(pl.multiple_of(i * step, step), step)
        block = cache_ref[rows, :]
        high, low = split(block)
        kcat[rows, 0:width] = high
        kcat[rows, width : 2 * width] = low
        turned = block.T
        t_high, t_low = split(turned)
        vt_hi[:, rows] = t_high
        vt_lo[:, rows] = t_low
        rope = rope_ref[:, rows].T
        r_high = rope.astype(jnp.bfloat16).astype(jnp.float32)
        r_low = rope - r_high
        wide = jnp.concatenate([r_high, r_high, r_low, jnp.zeros_like(rope)], axis=1)
        kcat[rows, 2 * width : 2 * width + 4 * rope.shape[1]] = wide.astype(jnp.bfloat16)
        return 0

    lax.fori_loop(0, cells // step, body, 0)


def rope_rows(aux, heads):
    packed = aux[0:heads, :] * FACTOR
    high = packed.astype(jnp.bfloat16).astype(jnp.float32)
    low = packed - high
    half = packed.shape[1] // 2
    blank = jnp.zeros((heads, half), jnp.float32)
    rows = []
    for part in (slice(0, half), slice(half, 2 * half)):
        rows.append(jnp.concatenate([high[:, part], low[:, part], high[:, part], blank], axis=1))
    return jnp.concatenate(rows, axis=0).astype(jnp.bfloat16)


def visit(parts, kcat, vt_hi, vt_lo, s_ref, ph_ref, pl_ref, window):
    cells = kcat.shape[0]
    width = vt_hi.shape[0]
    heads = parts[0][1].shape[0] - 8
    query = jnp.concatenate([p[0] for p in parts], axis=0) * FACTOR
    q_hi, q_lo = split(query)
    rope = jnp.concatenate([rope_rows(p[1], heads) for p in parts], axis=0)
    q_cat = jnp.concatenate([q_hi, q_hi, rope], axis=1)
    starts = jnp.concatenate([p[1][heads : heads + 1, :] - p[2] for p in parts], axis=1)
    extents = jnp.concatenate([p[1][heads + 1 : heads + 2, :] * p[3] for p in parts], axis=1)
    ends = starts + extents
    wrapped = ends - window
    count = query.shape[0]
    peak = jnp.full((1, count), FLOOR, jnp.float32)
    for c in range(cells // CHUNK):
        rows = slice(c * CHUNK, (c + 1) * CHUNK)
        scores = lax.dot_general(kcat[rows, :], q_cat, NT, preferred_element_type=jnp.float32)
        scores += lax.dot_general(
            kcat[rows, 0:width], q_lo, NT, preferred_element_type=jnp.float32
        )
        cell = lax.broadcasted_iota(jnp.int32, (CHUNK, count), 0).astype(jnp.float32) + c * CHUNK
        live = ((cell >= starts) & (cell < ends)) | (cell < wrapped)
        scores = jnp.where(live, scores, DEAD)
        s_ref[rows, 0:count] = scores
        peak = jnp.maximum(peak, jnp.max(scores, axis=0, keepdims=True))
    total = jnp.zeros((1, count), jnp.float32)
    summed = None
    for c in range(cells // CHUNK):
        rows = slice(c * CHUNK, (c + 1) * CHUNK)
        weights = jnp.exp2(s_ref[rows, 0:count] - peak)
        total += jnp.sum(weights, axis=0, keepdims=True)
        high, low = split(weights)
        ph_ref[rows, 0:count] = high
        pl_ref[rows, 0:count] = low
    high = ph_ref[:, 0:count]
    summed = jnp.dot(vt_hi[...], high, preferred_element_type=jnp.float32)
    summed += jnp.dot(vt_hi[...], pl_ref[:, 0:count], preferred_element_type=jnp.float32)
    summed += jnp.dot(vt_lo[...], high, preferred_element_type=jnp.float32)
    return summed, peak, total


def window_kernel(
    size,
    q_ref, aux_ref, cache_ref, rope_ref, out_ref,
    kcat, vt_hi, vt_lo, s_ref, ph_ref, pl_ref,
    q_got, aux_got, sums, stats, sums_got, stats_got,
    q_send, q_recv, a_send, a_recv, o_send, o_recv, t_send, t_recv,
):
    me = lax.axis_index("blk")
    cells = cache_ref.shape[0]
    window = (2 * HOPS + 1) * cells
    distances = [sign * k for k in range(1, HOPS + 1) for sign in (1, -1)]

    def device(distance):
        return {"blk": lax.rem(me + distance + size, size)}

    barrier = pltpu.get_barrier_semaphore()
    for d in distances:
        pl.semaphore_signal(barrier, inc=1, device_id=device(d), device_id_type=MESH)
    pl.semaphore_wait(barrier, 2 * HOPS)

    sent = []
    for i, d in enumerate(distances):
        for source, target, send, recv in (
            (q_ref, q_got, q_send, q_recv),
            (aux_ref, aux_got, a_send, a_recv),
        ):
            copy = pltpu.make_async_remote_copy(
                src_ref=source, dst_ref=target.at[i], send_sem=send.at[i], recv_sem=recv.at[i],
                device_id=device(d), device_id_type=MESH,
            )
            copy.start()
            sent.append(copy)

    prepare_cache(cache_ref, rope_ref, kcat, vt_hi, vt_lo)
    run = functools.partial(
        visit, kcat=kcat, vt_hi=vt_hi, vt_lo=vt_lo, s_ref=s_ref, ph_ref=ph_ref, pl_ref=pl_ref,
        window=window,
    )
    rows = q_ref.shape[0]
    own = run([(q_ref[...], aux_ref[...], float(HOPS * cells), 1.0)])
    sums[2 * HOPS, :, :] = own[0]
    stats[2 * HOPS, 0:1, :] = own[1]
    stats[2 * HOPS, 1:2, :] = own[2]

    def pair(k, _):
        parts = []
        for j, sign in ((0, 1), (1, -1)):
            i = 2 * k + j
            for source, target, send, recv in (
                (q_ref, q_got, q_send, q_recv),
                (aux_ref, aux_got, a_send, a_recv),
            ):
                pltpu.make_async_remote_copy(
                    src_ref=source, dst_ref=target.at[i], send_sem=send.at[i], recv_sem=recv.at[i],
                    device_id=device(1), device_id_type=MESH,
                ).wait_recv()
            slot = HOPS + sign * (k + 1)
            parts.append((q_got[i], aux_got[i], (slot * cells).astype(jnp.float32), 1.0))
        summed, peak, total = run(parts)
        for j, sign in ((0, 1), (1, -1)):
            i = 2 * k + j
            lanes = slice(j * rows, (j + 1) * rows)
            sums[i, :, :] = summed[:, lanes]
            stats[i, 0:1, :] = peak[:, lanes]
            stats[i, 1:2, :] = total[:, lanes]
            for source, target, send, recv in (
                (sums, sums_got, o_send, o_recv),
                (stats, stats_got, t_send, t_recv),
            ):
                pltpu.make_async_remote_copy(
                    src_ref=source.at[i], dst_ref=target.at[i],
                    send_sem=send.at[i], recv_sem=recv.at[i],
                    device_id=device(-sign * (k + 1)), device_id_type=MESH,
                ).start()
        return 0

    lax.fori_loop(0, HOPS, pair, 0)

    for i in range(2 * HOPS):
        for source, target, send, recv in (
            (sums, sums_got, o_send, o_recv),
            (stats, stats_got, t_send, t_recv),
        ):
            copy = pltpu.make_async_remote_copy(
                src_ref=source.at[i], dst_ref=target.at[i],
                send_sem=send.at[i], recv_sem=recv.at[i],
                device_id=device(1), device_id_type=MESH,
            )
            copy.wait_recv()
            copy.wait_send()

    for copy in sent:
        copy.wait_send()

    peak = stats[2 * HOPS, 0:1, :]
    for i in range(2 * HOPS):
        peak = jnp.maximum(peak, stats_got[i, 0:1, :])
    factors = [jnp.exp2(stats[2 * HOPS, 0:1, :] - peak)]
    total = stats[2 * HOPS, 1:2, :] * factors[0]
    for i in range(2 * HOPS):
        factors.append(jnp.exp2(stats_got[i, 0:1, :] - peak))
        total += stats_got[i, 1:2, :] * factors[i + 1]
    width = sums.shape[1]
    for c in range(0, width, 128):
        piece = sums[2 * HOPS, c : c + 128, :] * factors[0]
        for i in range(2 * HOPS):
            piece += sums_got[i, c : c + 128, :] * factors[i + 1]
        out_ref[:, c : c + 128] = (piece / total).T


def line_kernel(
    size,
    q_ref, aux_ref, cache_hbm, rope_ref, out_ref,
    kcat, vt_hi, vt_lo, s_ref, ph_ref, pl_ref,
    cache, q_all, aux_all, acc, across, across_got, along_got,
    fetch_sem, own_sem,
    qz_s, qz_r, az_s, az_r, qa_s, qa_r, qy_s, qy_r, ay_s, ay_r, early_s,
    oy_s, oy_r, oz_s, oz_r,
):
    me = lax.axis_index("blk")
    count = size // 2
    z, y = me // 2, lax.rem(me, 2)
    cells, width = cache.shape
    rows = q_ref.shape[0]
    window = (2 * HOPS + 1) * cells
    partner = {"blk": me + 1 - 2 * y}

    def at(zz):
        return {"blk": 2 * zz + y}

    def remote(source, target, send, recv, device):
        return pltpu.make_async_remote_copy(
            src_ref=source, dst_ref=target, send_sem=send, recv_sem=recv,
            device_id=device, device_id_type=MESH,
        )

    def source_row(j):
        near = jnp.minimum(z, count - 1 - z)
        both = j < 2 * near
        distance = jnp.where(both, j // 2 + 1, j - near + 1)
        upward = jnp.where(both, lax.rem(j, 2) == 0, z < count - 1 - z)
        return jnp.where(upward, z + distance, z - distance)

    def q_along(zz, side):
        target = at(lax.rem(z + 1 - 2 * side + count, count))
        return (
            remote(q_all.at[zz, 0], q_all.at[zz, 0], qz_s.at[side, zz], qz_r.at[zz], target),
            remote(aux_all.at[zz, 0], aux_all.at[zz, 0], az_s.at[side, zz], az_r.at[zz], target),
        )

    early_rows, late_rows = pl.ds(0, EARLY), pl.ds(EARLY, rows - EARLY)

    def early_along(zz, side):
        piece = q_all.at[zz, 1, early_rows]
        target = at(lax.rem(z + 1 - 2 * side + count, count))
        return remote(piece, piece, qa_s.at[side, zz], qa_r.at[zz], target)

    def q_across(zz):
        return (
            remote(
                q_all.at[zz, 0, late_rows], q_all.at[zz, 1, late_rows],
                qy_s.at[zz], qy_r.at[zz], partner,
            ),
            remote(aux_all.at[zz, 0], aux_all.at[zz, 1], ay_s.at[zz], ay_r.at[zz], partner),
        )

    def early_across():
        return remote(
            q_all.at[z, 0, early_rows], q_all.at[z, 1, early_rows], early_s.at[0], qa_r.at[z],
            partner,
        )

    half = width // 2

    def sum_across(zz, h):
        return remote(
            across.at[zz, h], across_got.at[zz, h], oy_s.at[zz, h], oy_r.at[zz, h], partner
        )

    def sum_along(zz, h):
        return remote(acc.at[zz, h], along_got.at[z, h], oz_s.at[zz, h], oz_r.at[z, h], at(zz))

    def sum_straight(zz, h):
        device = {"blk": 2 * zz + 1 - y}
        return remote(across.at[zz, h], along_got.at[z, h], oz_s.at[zz, h], oz_r.at[z, h], device)

    def sum_from(zz, h):
        return remote(acc.at[zz, h], along_got.at[zz, h], oz_s.at[zz, h], oz_r.at[zz, h], at(zz))

    def opposite(zz):
        return 2 * jnp.abs(z - zz) == count

    def fetch(i):
        part = pl.ds(pl.multiple_of(i * STEP, STEP), STEP)
        return pltpu.make_async_copy(cache_hbm.at[part], cache.at[part], fetch_sem.at[i])

    own_copies = (
        pltpu.make_async_copy(q_ref, q_all.at[z, 0], own_sem.at[0]),
        pltpu.make_async_copy(aux_ref, aux_all.at[z, 0], own_sem.at[1]),
    )
    for copy in own_copies:
        copy.start()
    for i in range(cells // STEP):
        fetch(i).start()

    barrier = pltpu.get_barrier_semaphore()
    pl.semaphore_signal(barrier, inc=1, device_id=partner, device_id_type=MESH)
    for k in range(1, count):
        other = at(lax.rem(z + k, count))
        pl.semaphore_signal(barrier, inc=1, device_id=other, device_id_type=MESH)
    for copy in own_copies:
        copy.wait()
    pl.semaphore_wait(barrier, count)

    def sides(zz, action):
        @pl.when((z < count - 1) & (zz <= z))
        def _():
            action(0)

        @pl.when((z > 0) & (zz >= z))
        def _():
            action(1)

    def start_along(side, zz):
        for copy in q_along(zz, side):
            copy.start()

    early_across().start()
    sides(z, functools.partial(start_along, zz=z))
    for copy in q_across(z):
        copy.start()

    prepare_cache(cache, rope_ref, kcat, vt_hi, vt_lo, fetch)
    early_across().wait_recv()
    sides(z, lambda side: early_along(z, side).start())

    def pass_on(zz):
        for copy in q_along(zz, 0):
            copy.wait_recv()
        sides(zz, functools.partial(start_along, zz=zz))
        for copy in q_across(zz):
            copy.start()
        early_along(zz, 0).wait_recv()
        sides(zz, lambda side: early_along(zz, side).start())

    def compute(zz):
        for copy in q_across(zz):
            copy.wait_recv()
        parts = []
        for c in range(2):
            block = 2 * zz + (y if c == 0 else 1 - y)
            slot = lax.rem(me - block + HOPS + size, size)
            alive = jnp.where(slot <= 2 * HOPS, 1.0, 0.0).astype(jnp.float32)
            parts.append((q_all[zz, c], aux_all[zz, c], (slot * cells).astype(jnp.float32), alive))
        summed, peak, total = visit(
            parts, kcat, vt_hi, vt_lo, s_ref, ph_ref, pl_ref, window
        )
        for ref, lanes in ((across, slice(rows, 2 * rows)), (acc, slice(0, rows))):
            extra = jnp.concatenate(
                [peak[:, lanes], total[:, lanes], jnp.zeros((6, rows), jnp.float32)], axis=0
            )
            for h in range(2):
                ref[zz, h, 0:half, :] = summed[h * half : (h + 1) * half, lanes]
                ref[zz, h, half : half + 8, :] = extra

        @pl.when(opposite(zz))
        def _():
            for h in range(2):
                sum_straight(zz, h).start()

        @pl.when(jnp.logical_not(opposite(zz)))
        def _():
            for h in range(2):
                sum_across(zz, h).start()

    def merge(zz, got, k, h):
        first, second = acc[zz, h, half : half + 1, :], got[k, h, half : half + 1, :]
        peak = jnp.maximum(first, second)
        first, second = jnp.exp2(first - peak), jnp.exp2(second - peak)
        total = acc[zz, h, half + 1 : half + 2, :] * first
        total += got[k, h, half + 1 : half + 2, :] * second
        acc[zz, h, 0:half, :] = acc[zz, h, 0:half, :] * first + got[k, h, 0:half, :] * second
        acc[zz, h, half : half + 1, :] = peak
        acc[zz, h, half + 1 : half + 2, :] = total

    def step(i, _):
        @pl.when(i < count - 1)
        def _():
            pass_on(source_row(i))

        @pl.when(i < count)
        def _():
            compute(jnp.where(i == 0, z, source_row(i - 1)))

        @pl.when(i >= 1)
        def _():
            zz = jnp.where(i == 1, z, source_row(i - 2))

            @pl.when(jnp.logical_not(opposite(zz)))
            def _():
                for h in range(2):
                    sum_across(zz, h).wait_recv()
                    merge(zz, across_got, zz, h)

                    @pl.when(i >= 2)
                    def _():
                        sum_along(zz, h).start()

        return 0

    lax.fori_loop(0, count + 1, step, 0)

    def gather(j, _):
        zz = source_row(j)
        for h in range(2):
            sum_from(zz, h).wait_recv()
            merge(z, along_got, zz, h)
        return 0

    lax.fori_loop(0, count - 1, gather, 0)
    total = acc[z, 0, half + 1 : half + 2, :]
    for c in range(0, width, 128):
        h, r = divmod(c, half)
        out_ref[:, c : c + 128] = (acc[z, h, r : r + 128, :] / total).T

    def finish(side, zz):
        for copy in q_along(zz, side):
            copy.wait_send()
        early_along(zz, side).wait_send()

    early_across().wait_send()
    for k in range(count):
        zz = lax.rem(z + k, count)
        sides(zz, functools.partial(finish, zz=zz))
        for copy in q_across(zz):
            copy.wait_send()

        @pl.when(opposite(zz))
        def _():
            for h in range(2):
                sum_straight(zz, h).wait_send()

        @pl.when(jnp.logical_not(opposite(zz)))
        def _():
            for h in range(2):
                sum_across(zz, h).wait_send()
                if k > 0:
                    sum_along(zz, h).wait_send()


def pack_aux(q_rope, home_offset, lengths):
    height, heads, rope = q_rope.shape
    packed = jnp.concatenate([q_rope[i] for i in range(height)], axis=1)
    meta = jnp.stack([home_offset, lengths]).astype(jnp.float32)
    meta = jnp.repeat(meta, heads, axis=1)
    return jnp.concatenate([packed, meta, jnp.zeros((6, height * heads), jnp.float32)], axis=0)


def shards(size, q_latent, q_rope, cache_latent, cache_rope, home_offset, lengths):
    height, heads, width = q_latent.shape
    cells, rope = cache_rope.shape
    rows = height * heads
    aux = pack_aux(q_rope, home_offset, lengths)
    flat = q_latent.reshape(rows, width)
    rope_turned = cache_rope.T
    dma = pltpu.SemaphoreType.DMA
    vmem, anywhere = (pl.BlockSpec(memory_space=m) for m in (pltpu.VMEM, pl.ANY))
    working = [
        pltpu.VMEM((cells, 2 * width + 4 * rope), jnp.bfloat16),
        pltpu.VMEM((width, cells), jnp.bfloat16),
        pltpu.VMEM((width, cells), jnp.bfloat16),
        pltpu.VMEM((cells, 2 * rows), jnp.float32),
        pltpu.VMEM((cells, 2 * rows), jnp.bfloat16),
        pltpu.VMEM((cells, 2 * rows), jnp.bfloat16),
    ]
    if size == 2 * HOPS + 2:
        kernel = line_kernel
        n = size // 2
        in_specs = [anywhere, anywhere, anywhere, vmem]
        scratch = [
            pltpu.VMEM((cells, width), jnp.float32),
            pltpu.VMEM((n, 2, rows, width), jnp.float32),
            pltpu.VMEM((n, 2, heads + 8, rows), jnp.float32),
        ]
        scratch += [pltpu.VMEM((n, 2, width // 2 + 8, rows), jnp.float32)] * 4
        scratch += [dma((cells // STEP,)), dma((2,))]
        scratch += [dma((2, n)), dma((n,))] * 3 + [dma((n,))] * 4 + [dma((1,))] + [dma((n, 2))] * 4
    else:
        kernel = window_kernel
        n = 2 * HOPS
        in_specs = [vmem] * 4
        scratch = [
            pltpu.VMEM((n, rows, width), jnp.float32),
            pltpu.VMEM((n, heads + 8, rows), jnp.float32),
            pltpu.VMEM((n + 1, width, rows), jnp.float32),
            pltpu.VMEM((n + 1, 8, rows), jnp.float32),
            pltpu.VMEM((n, width, rows), jnp.float32),
            pltpu.VMEM((n, 8, rows), jnp.float32),
        ] + [dma((n,))] * 8
    out = pl.pallas_call(
        functools.partial(kernel, size),
        out_shape=jax.ShapeDtypeStruct((rows, width), jnp.float32),
        in_specs=in_specs,
        out_specs=vmem,
        scratch_shapes=working + scratch,
        compiler_params=pltpu.CompilerParams(
            collective_id=0, has_side_effects=True, vmem_limit_bytes=60 * 1024 * 1024
        ),
    )(flat, aux, cache_latent, rope_turned)
    return out.reshape(height, heads, width)


def solution(mesh):
    return jax.shard_map(
        functools.partial(shards, mesh.shape["blk"]),
        mesh=mesh,
        in_specs=(
            P(("groups", "blk"), "head", None),
            P(("groups", "blk"), "head", None),
            P(("groups", "blk"), None),
            P(("groups", "blk"), None),
            P(("groups", "blk")),
            P(("groups", "blk")),
        ),
        out_specs=P(("groups", "blk"), "head", None),
        check_vma=False,
    )
```

```python
import functools
import math

import jax
import jax.numpy as jnp
from jax import lax
from jax.experimental import pallas as pl
from jax.experimental.pallas import tpu as pltpu
from jax.sharding import PartitionSpec as P

ROPE = 64
NOPE = 128
HOPS = 3

MESH = pl.DeviceIdType.MESH
FLOOR = -1e30
DEAD = -2e30
FACTOR = math.log2(math.e) / math.sqrt(NOPE + ROPE)
CHUNK = 256
STEP = 256
EARLY = 64

NT = (((1,), (1,)), ((), ()))


def split(x):
    high = x.astype(jnp.bfloat16)
    low = (x - high.astype(jnp.float32)).astype(jnp.bfloat16)
    return high, low


def prepare_cache(cache_ref, rope_ref, kcat, vt_hi, vt_lo, fetch=None):
    cells, width = cache_ref.shape
    step = STEP

    def body(i, _):
        if fetch is not None:
            fetch(i).wait()
        rows = pl.ds(pl.multiple_of(i * step, step), step)
        block = cache_ref[rows, :]
        high, low = split(block)
        kcat[rows, 0:width] = high
        kcat[rows, width : 2 * width] = low
        turned = block.T
        t_high, t_low = split(turned)
        vt_hi[:, rows] = t_high
        vt_lo[:, rows] = t_low
        rope = rope_ref[:, rows].T
        r_high = rope.astype(jnp.bfloat16).astype(jnp.float32)
        r_low = rope - r_high
        wide = jnp.concatenate([r_high, r_high, r_low, jnp.zeros_like(rope)], axis=1)
        kcat[rows, 2 * width : 2 * width + 4 * rope.shape[1]] = wide.astype(jnp.bfloat16)
        return 0

    lax.fori_loop(0, cells // step, body, 0)


def rope_rows(aux, heads):
    packed = aux[0:heads, :] * FACTOR
    high = packed.astype(jnp.bfloat16).astype(jnp.float32)
    low = packed - high
    half = packed.shape[1] // 2
    blank = jnp.zeros((heads, half), jnp.float32)
    rows = []
    for part in (slice(0, half), slice(half, 2 * half)):
        rows.append(jnp.concatenate([high[:, part], low[:, part], high[:, part], blank], axis=1))
    return jnp.concatenate(rows, axis=0).astype(jnp.bfloat16)


def visit(parts, kcat, vt_hi, vt_lo, s_ref, ph_ref, pl_ref, window):
    cells = kcat.shape[0]
    width = vt_hi.shape[0]
    heads = parts[0][1].shape[0] - 8
    query = jnp.concatenate([p[0] for p in parts], axis=0) * FACTOR
    q_hi, q_lo = split(query)
    rope = jnp.concatenate([rope_rows(p[1], heads) for p in parts], axis=0)
    q_cat = jnp.concatenate([q_hi, q_hi, rope], axis=1)
    starts = jnp.concatenate([p[1][heads : heads + 1, :] - p[2] for p in parts], axis=1)
    extents = jnp.concatenate([p[1][heads + 1 : heads + 2, :] * p[3] for p in parts], axis=1)
    ends = starts + extents
    wrapped = ends - window
    count = query.shape[0]
    peak = jnp.full((1, count), FLOOR, jnp.float32)
    for c in range(cells // CHUNK):
        rows = slice(c * CHUNK, (c + 1) * CHUNK)
        scores = lax.dot_general(kcat[rows, :], q_cat, NT, preferred_element_type=jnp.float32)
        scores += lax.dot_general(
            kcat[rows, 0:width], q_lo, NT, preferred_element_type=jnp.float32
        )
        cell = lax.broadcasted_iota(jnp.int32, (CHUNK, count), 0).astype(jnp.float32) + c * CHUNK
        live = ((cell >= starts) & (cell < ends)) | (cell < wrapped)
        scores = jnp.where(live, scores, DEAD)
        s_ref[rows, 0:count] = scores
        peak = jnp.maximum(peak, jnp.max(scores, axis=0, keepdims=True))
    total = jnp.zeros((1, count), jnp.float32)
    summed = None
    for c in range(cells // CHUNK):
        rows = slice(c * CHUNK, (c + 1) * CHUNK)
        weights = jnp.exp2(s_ref[rows, 0:count] - peak)
        total += jnp.sum(weights, axis=0, keepdims=True)
        high, low = split(weights)
        ph_ref[rows, 0:count] = high
        pl_ref[rows, 0:count] = low
    high = ph_ref[:, 0:count]
    summed = jnp.dot(vt_hi[...], high, preferred_element_type=jnp.float32)
    summed += jnp.dot(vt_hi[...], pl_ref[:, 0:count], preferred_element_type=jnp.float32)
    summed += jnp.dot(vt_lo[...], high, preferred_element_type=jnp.float32)
    return summed, peak, total


def window_kernel(
    size,
    q_ref, aux_ref, cache_ref, rope_ref, out_ref,
    kcat, vt_hi, vt_lo, s_ref, ph_ref, pl_ref,
    q_got, aux_got, sums, stats, sums_got, stats_got,
    q_send, q_recv, a_send, a_recv, o_send, o_recv, t_send, t_recv,
):
    me = lax.axis_index("blk")
    cells = cache_ref.shape[0]
    window = (2 * HOPS + 1) * cells
    distances = [sign * k for k in range(1, HOPS + 1) for sign in (1, -1)]

    def device(distance):
        return {"blk": lax.rem(me + distance + size, size)}

    barrier = pltpu.get_barrier_semaphore()
    for d in distances:
        pl.semaphore_signal(barrier, inc=1, device_id=device(d), device_id_type=MESH)
    pl.semaphore_wait(barrier, 2 * HOPS)

    sent = []
    for i, d in enumerate(distances):
        for source, target, send, recv in (
            (q_ref, q_got, q_send, q_recv),
            (aux_ref, aux_got, a_send, a_recv),
        ):
            copy = pltpu.make_async_remote_copy(
                src_ref=source, dst_ref=target.at[i], send_sem=send.at[i], recv_sem=recv.at[i],
                device_id=device(d), device_id_type=MESH,
            )
            copy.start()
            sent.append(copy)

    prepare_cache(cache_ref, rope_ref, kcat, vt_hi, vt_lo)
    run = functools.partial(
        visit, kcat=kcat, vt_hi=vt_hi, vt_lo=vt_lo, s_ref=s_ref, ph_ref=ph_ref, pl_ref=pl_ref,
        window=window,
    )
    rows = q_ref.shape[0]
    own = run([(q_ref[...], aux_ref[...], float(HOPS * cells), 1.0)])
    sums[2 * HOPS, :, :] = own[0]
    stats[2 * HOPS, 0:1, :] = own[1]
    stats[2 * HOPS, 1:2, :] = own[2]

    def pair(k, _):
        parts = []
        for j, sign in ((0, 1), (1, -1)):
            i = 2 * k + j
            for source, target, send, recv in (
                (q_ref, q_got, q_send, q_recv),
                (aux_ref, aux_got, a_send, a_recv),
            ):
                pltpu.make_async_remote_copy(
                    src_ref=source, dst_ref=target.at[i], send_sem=send.at[i], recv_sem=recv.at[i],
                    device_id=device(1), device_id_type=MESH,
                ).wait_recv()
            slot = HOPS + sign * (k + 1)
            parts.append((q_got[i], aux_got[i], (slot * cells).astype(jnp.float32), 1.0))
        summed, peak, total = run(parts)
        for j, sign in ((0, 1), (1, -1)):
            i = 2 * k + j
            lanes = slice(j * rows, (j + 1) * rows)
            sums[i, :, :] = summed[:, lanes]
            stats[i, 0:1, :] = peak[:, lanes]
            stats[i, 1:2, :] = total[:, lanes]
            for source, target, send, recv in (
                (sums, sums_got, o_send, o_recv),
                (stats, stats_got, t_send, t_recv),
            ):
                pltpu.make_async_remote_copy(
                    src_ref=source.at[i], dst_ref=target.at[i],
                    send_sem=send.at[i], recv_sem=recv.at[i],
                    device_id=device(-sign * (k + 1)), device_id_type=MESH,
                ).start()
        return 0

    lax.fori_loop(0, HOPS, pair, 0)

    for i in range(2 * HOPS):
        for source, target, send, recv in (
            (sums, sums_got, o_send, o_recv),
            (stats, stats_got, t_send, t_recv),
        ):
            copy = pltpu.make_async_remote_copy(
                src_ref=source.at[i], dst_ref=target.at[i],
                send_sem=send.at[i], recv_sem=recv.at[i],
                device_id=device(1), device_id_type=MESH,
            )
            copy.wait_recv()
            copy.wait_send()

    for copy in sent:
        copy.wait_send()

    peak = stats[2 * HOPS, 0:1, :]
    for i in range(2 * HOPS):
        peak = jnp.maximum(peak, stats_got[i, 0:1, :])
    factors = [jnp.exp2(stats[2 * HOPS, 0:1, :] - peak)]
    total = stats[2 * HOPS, 1:2, :] * factors[0]
    for i in range(2 * HOPS):
        factors.append(jnp.exp2(stats_got[i, 0:1, :] - peak))
        total += stats_got[i, 1:2, :] * factors[i + 1]
    width = sums.shape[1]
    for c in range(0, width, 128):
        piece = sums[2 * HOPS, c : c + 128, :] * factors[0]
        for i in range(2 * HOPS):
            piece += sums_got[i, c : c + 128, :] * factors[i + 1]
        out_ref[:, c : c + 128] = (piece / total).T


def line_kernel(
    size,
    q_ref, aux_ref, cache_hbm, rope_ref, out_ref,
    kcat, vt_hi, vt_lo, s_ref, ph_ref, pl_ref,
    cache, q_all, aux_all, acc, across, across_got, along_got,
    fetch_sem, own_sem,
    qz_s, qz_r, qe_s, qe_r, az_s, az_r, qa_s, qa_r, qy_s, qy_r, ay_s, ay_r, early_s,
    oy_s, oy_r, oz_s, oz_r,
):
    me = lax.axis_index("blk")
    count = size // 2
    z, y = me // 2, lax.rem(me, 2)
    cells, width = cache.shape
    rows = q_ref.shape[0]
    window = (2 * HOPS + 1) * cells
    partner = {"blk": me + 1 - 2 * y}

    def at(zz):
        return {"blk": 2 * zz + y}

    def remote(source, target, send, recv, device):
        return pltpu.make_async_remote_copy(
            src_ref=source, dst_ref=target, send_sem=send, recv_sem=recv,
            device_id=device, device_id_type=MESH,
        )

    def source_row(j):
        near = jnp.minimum(z, count - 1 - z)
        both = j < 2 * near
        distance = jnp.where(both, j // 2 + 1, j - near + 1)
        upward = jnp.where(both, lax.rem(j, 2) == 0, z < count - 1 - z)
        return jnp.where(upward, z + distance, z - distance)

    early_rows, late_rows = pl.ds(0, EARLY), pl.ds(EARLY, rows - EARLY)

    def q_along(zz, side):
        target = at(lax.rem(z + 1 - 2 * side + count, count))
        piece = q_all.at[zz, 0, late_rows]
        return (
            remote(piece, piece, qz_s.at[side, zz], qz_r.at[zz], target),
            remote(aux_all.at[zz, 0], aux_all.at[zz, 0], az_s.at[side, zz], az_r.at[zz], target),
        )

    def rest_along(zz, side):
        target = at(lax.rem(z + 1 - 2 * side + count, count))
        piece = q_all.at[zz, 0, early_rows]
        return remote(piece, piece, qe_s.at[side, zz], qe_r.at[zz], target)

    def early_along(zz, side):
        piece = q_all.at[zz, 1, early_rows]
        target = at(lax.rem(z + 1 - 2 * side + count, count))
        return remote(piece, piece, qa_s.at[side, zz], qa_r.at[zz], target)

    def q_across(zz):
        return (
            remote(
                q_all.at[zz, 0, late_rows], q_all.at[zz, 1, late_rows],
                qy_s.at[zz], qy_r.at[zz], partner,
            ),
            remote(aux_all.at[zz, 0], aux_all.at[zz, 1], ay_s.at[zz], ay_r.at[zz], partner),
        )

    def early_across():
        return remote(
            q_all.at[z, 0, early_rows], q_all.at[z, 1, early_rows], early_s.at[0], qa_r.at[z],
            partner,
        )

    half = width // 2

    def sum_across(zz, h):
        return remote(
            across.at[zz, h], across_got.at[zz, h], oy_s.at[zz, h], oy_r.at[zz, h], partner
        )

    def sum_along(zz, h):
        return remote(acc.at[zz, h], along_got.at[z, h], oz_s.at[zz, h], oz_r.at[z, h], at(zz))

    def sum_straight(zz, h):
        device = {"blk": 2 * zz + 1 - y}
        return remote(across.at[zz, h], along_got.at[z, h], oz_s.at[zz, h], oz_r.at[z, h], device)

    def sum_from(zz, h):
        return remote(acc.at[zz, h], along_got.at[zz, h], oz_s.at[zz, h], oz_r.at[zz, h], at(zz))

    def opposite(zz):
        return 2 * jnp.abs(z - zz) == count

    def fetch(i):
        part = pl.ds(pl.multiple_of(i * STEP, STEP), STEP)
        return pltpu.make_async_copy(cache_hbm.at[part], cache.at[part], fetch_sem.at[i])

    own_copies = (
        pltpu.make_async_copy(q_ref, q_all.at[z, 0], own_sem.at[0]),
        pltpu.make_async_copy(aux_ref, aux_all.at[z, 0], own_sem.at[1]),
    )
    for copy in own_copies:
        copy.start()
    for i in range(cells // STEP):
        fetch(i).start()

    barrier = pltpu.get_barrier_semaphore()
    pl.semaphore_signal(barrier, inc=1, device_id=partner, device_id_type=MESH)
    for k in range(1, count):
        other = at(lax.rem(z + k, count))
        pl.semaphore_signal(barrier, inc=1, device_id=other, device_id_type=MESH)
    for copy in own_copies:
        copy.wait()
    pl.semaphore_wait(barrier, count)

    def sides(zz, action):
        @pl.when((z < count - 1) & (zz <= z))
        def _():
            action(0)

        @pl.when((z > 0) & (zz >= z))
        def _():
            action(1)

    def unused(zz, row):
        return (2 * jnp.abs(row - zz) == count) & ((row == 0) | (row == count - 1))

    def rest_sides(zz, action):
        def guarded(side):
            @pl.when(jnp.logical_not(unused(zz, z + 1 - 2 * side)))
            def _():
                action(side)

        sides(zz, guarded)

    def start_along(side, zz):
        for copy in q_along(zz, side):
            copy.start()

    early_across().start()
    sides(z, functools.partial(start_along, zz=z))
    for copy in q_across(z):
        copy.start()
    rest_sides(z, lambda side: rest_along(z, side).start())

    prepare_cache(cache, rope_ref, kcat, vt_hi, vt_lo, fetch)
    early_across().wait_recv()
    sides(z, lambda side: early_along(z, side).start())

    def pass_on(zz):
        for copy in q_along(zz, 0):
            copy.wait_recv()
        sides(zz, functools.partial(start_along, zz=zz))
        for copy in q_across(zz):
            copy.start()

        @pl.when(jnp.logical_not(unused(zz, z)))
        def _():
            rest_along(zz, 0).wait_recv()
            rest_sides(zz, lambda side: rest_along(zz, side).start())

        early_along(zz, 0).wait_recv()
        sides(zz, lambda side: early_along(zz, side).start())

    def compute(zz):
        for copy in q_across(zz):
            copy.wait_recv()
        parts = []
        for c in range(2):
            block = 2 * zz + (y if c == 0 else 1 - y)
            slot = lax.rem(me - block + HOPS + size, size)
            alive = jnp.where(slot <= 2 * HOPS, 1.0, 0.0).astype(jnp.float32)
            parts.append((q_all[zz, c], aux_all[zz, c], (slot * cells).astype(jnp.float32), alive))
        summed, peak, total = visit(
            parts, kcat, vt_hi, vt_lo, s_ref, ph_ref, pl_ref, window
        )
        for ref, lanes in ((across, slice(rows, 2 * rows)), (acc, slice(0, rows))):
            extra = jnp.concatenate(
                [peak[:, lanes], total[:, lanes], jnp.zeros((6, rows), jnp.float32)], axis=0
            )
            for h in range(2):
                ref[zz, h, 0:half, :] = summed[h * half : (h + 1) * half, lanes]
                ref[zz, h, half : half + 8, :] = extra

        @pl.when(opposite(zz))
        def _():
            for h in range(2):
                sum_straight(zz, h).start()

        @pl.when(jnp.logical_not(opposite(zz)))
        def _():
            for h in range(2):
                sum_across(zz, h).start()

    def merge(zz, got, k, h):
        first, second = acc[zz, h, half : half + 1, :], got[k, h, half : half + 1, :]
        peak = jnp.maximum(first, second)
        first, second = jnp.exp2(first - peak), jnp.exp2(second - peak)
        total = acc[zz, h, half + 1 : half + 2, :] * first
        total += got[k, h, half + 1 : half + 2, :] * second
        acc[zz, h, 0:half, :] = acc[zz, h, 0:half, :] * first + got[k, h, 0:half, :] * second
        acc[zz, h, half : half + 1, :] = peak
        acc[zz, h, half + 1 : half + 2, :] = total

    def step(i, _):
        @pl.when(i < count - 1)
        def _():
            pass_on(source_row(i))

        @pl.when(i < count)
        def _():
            compute(jnp.where(i == 0, z, source_row(i - 1)))

        @pl.when(i >= 1)
        def _():
            zz = jnp.where(i == 1, z, source_row(i - 2))

            @pl.when(jnp.logical_not(opposite(zz)))
            def _():
                for h in range(2):
                    sum_across(zz, h).wait_recv()
                    merge(zz, across_got, zz, h)

                    @pl.when(i >= 2)
                    def _():
                        sum_along(zz, h).start()

        return 0

    lax.fori_loop(0, count + 1, step, 0)

    def gather(j, _):
        zz = source_row(j)
        for h in range(2):
            sum_from(zz, h).wait_recv()
            merge(z, along_got, zz, h)
        return 0

    lax.fori_loop(0, count - 1, gather, 0)
    total = acc[z, 0, half + 1 : half + 2, :]
    for c in range(0, width, 128):
        h, r = divmod(c, half)
        out_ref[:, c : c + 128] = (acc[z, h, r : r + 128, :] / total).T

    def finish(side, zz):
        for copy in q_along(zz, side):
            copy.wait_send()
        early_along(zz, side).wait_send()

    early_across().wait_send()
    for k in range(count):
        zz = lax.rem(z + k, count)
        sides(zz, functools.partial(finish, zz=zz))
        rest_sides(zz, lambda side: rest_along(zz, side).wait_send())
        for copy in q_across(zz):
            copy.wait_send()

        @pl.when(opposite(zz))
        def _():
            for h in range(2):
                sum_straight(zz, h).wait_send()

        @pl.when(jnp.logical_not(opposite(zz)))
        def _():
            for h in range(2):
                sum_across(zz, h).wait_send()
                if k > 0:
                    sum_along(zz, h).wait_send()


def pack_aux(q_rope, home_offset, lengths):
    height, heads, rope = q_rope.shape
    packed = jnp.concatenate([q_rope[i] for i in range(height)], axis=1)
    meta = jnp.stack([home_offset, lengths]).astype(jnp.float32)
    meta = jnp.repeat(meta, heads, axis=1)
    return jnp.concatenate([packed, meta, jnp.zeros((6, height * heads), jnp.float32)], axis=0)


def shards(size, q_latent, q_rope, cache_latent, cache_rope, home_offset, lengths):
    height, heads, width = q_latent.shape
    cells, rope = cache_rope.shape
    rows = height * heads
    aux = pack_aux(q_rope, home_offset, lengths)
    flat = q_latent.reshape(rows, width)
    rope_turned = cache_rope.T
    dma = pltpu.SemaphoreType.DMA
    vmem, anywhere = (pl.BlockSpec(memory_space=m) for m in (pltpu.VMEM, pl.ANY))
    working = [
        pltpu.VMEM((cells, 2 * width + 4 * rope), jnp.bfloat16),
        pltpu.VMEM((width, cells), jnp.bfloat16),
        pltpu.VMEM((width, cells), jnp.bfloat16),
        pltpu.VMEM((cells, 2 * rows), jnp.float32),
        pltpu.VMEM((cells, 2 * rows), jnp.bfloat16),
        pltpu.VMEM((cells, 2 * rows), jnp.bfloat16),
    ]
    if size == 2 * HOPS + 2:
        kernel = line_kernel
        n = size // 2
        in_specs = [anywhere, anywhere, anywhere, vmem]
        scratch = [
            pltpu.VMEM((cells, width), jnp.float32),
            pltpu.VMEM((n, 2, rows, width), jnp.float32),
            pltpu.VMEM((n, 2, heads + 8, rows), jnp.float32),
        ]
        scratch += [pltpu.VMEM((n, 2, width // 2 + 8, rows), jnp.float32)] * 4
        scratch += [dma((cells // STEP,)), dma((2,))]
        scratch += [dma((2, n)), dma((n,))] * 4 + [dma((n,))] * 4 + [dma((1,))] + [dma((n, 2))] * 4
    else:
        kernel = window_kernel
        n = 2 * HOPS
        in_specs = [vmem] * 4
        scratch = [
            pltpu.VMEM((n, rows, width), jnp.float32),
            pltpu.VMEM((n, heads + 8, rows), jnp.float32),
            pltpu.VMEM((n + 1, width, rows), jnp.float32),
            pltpu.VMEM((n + 1, 8, rows), jnp.float32),
            pltpu.VMEM((n, width, rows), jnp.float32),
            pltpu.VMEM((n, 8, rows), jnp.float32),
        ] + [dma((n,))] * 8
    out = pl.pallas_call(
        functools.partial(kernel, size),
        out_shape=jax.ShapeDtypeStruct((rows, width), jnp.float32),
        in_specs=in_specs,
        out_specs=vmem,
        scratch_shapes=working + scratch,
        compiler_params=pltpu.CompilerParams(
            collective_id=0, has_side_effects=True, vmem_limit_bytes=60 * 1024 * 1024
        ),
    )(flat, aux, cache_latent, rope_turned)
    return out.reshape(height, heads, width)


def solution(mesh):
    return jax.shard_map(
        functools.partial(shards, mesh.shape["blk"]),
        mesh=mesh,
        in_specs=(
            P(("groups", "blk"), "head", None),
            P(("groups", "blk"), "head", None),
            P(("groups", "blk"), None),
            P(("groups", "blk"), None),
            P(("groups", "blk")),
            P(("groups", "blk")),
        ),
        out_specs=P(("groups", "blk"), "head", None),
        check_vma=False,
    )
```
